512 devices in a mesh: rep: 64 (over z_hi, y, core), fsdp: 8 (over x, z_lo).
Axes of the slice: x: 4, y: 8, z: 8 (z_hi: 4, z_lo: 2; z = z_hi * 2 + z_lo), core: 2. Of those that a mesh axis runs over, the one named last changes fastest.
Arguments:
- anchor: float32 [4096, 512], P('fsdp', 'rep'), may hold values from -6 to 6
- momentum: float32 [4096, 512], P('fsdp', 'rep'), may hold values from -1.2 to 1.2
- tokens: bfloat16 [64, 2048, 4096], P('rep', 'fsdp'), may hold values from -6 to 6
- targets: bfloat16 [64, 2048, 512], P('rep', 'fsdp'), may hold values from -6 to 6
- first_moment: float32 [64, 4096, 512], P('rep', 'fsdp'), may hold values from -0.0018 to 0.0018
- second_moment: float32 [64, 4096, 512], P('rep', 'fsdp'), may hold values from 2e-08 to 2e-07
Outputs:
- anchor_next: float32 [4096, 512], P('fsdp', 'rep')
- momentum_next: float32 [4096, 512], P('fsdp', 'rep')
The draws below stay inside these ranges and needn't reach their ends.
All inputs are finite; a program needn't handle non-finite values.
Results may differ from the reference program's by a relative error of at most 0.002.
Values may be sent and summed in bfloat16 or wider, within the bound.
No kernel may reach another device: no remote copies, remote signals or barrier semaphores. Data moves between devices by JAX's collectives and lax.ppermute only.
A program may use at most 64 MiB of HBM per device.

```python
import math
import jax
import jax.numpy as jnp
from jax import lax

D = 4096
KVW = 512
NTOK = 2048
REPS = 64
N_REP = 64
N_FSDP = 8


def steps_of(own_key, dims, cuts, smallest, high):
    loudness = 1.0
    for axis_at, parts in cuts:
        draws = jax.random.uniform(jax.random.fold_in(jax.random.fold_in(own_key, 6), axis_at), (parts,), jnp.float32, smallest / len(cuts), high / len(cuts))
        loudness = loudness * jnp.repeat(jnp.exp(draws), dims[axis_at] // parts).reshape((-1,) + (1,) * (len(dims) - 1 - axis_at))
    return loudness


def scatter_about(rng, extent, width, bound, pieces=(), dtype=jnp.bfloat16):
    array = width * jax.random.normal(rng, extent, jnp.float32)
    if pieces:
        array = array * steps_of(rng, extent, pieces, -0.22, 0.18)
    return jnp.clip(array, -bound, bound).astype(dtype)


def setup_inputs(seed: int = 0) -> dict:
    key_list = jax.random.split(jax.random.key(seed), 7)
    anchor = scatter_about(key_list[0], (D, KVW), 1.0, 6.0, ((0, 8), (1, 64)), jnp.float32)
    momentum = scatter_about(key_list[1], (D, KVW), 0.2, 1.2, ((0, 8), (1, 64)), jnp.float32)
    tokens = scatter_about(key_list[2], (REPS, NTOK, D), 1.0, 6.0, ((0, 64), (1, 8)))
    targets = scatter_about(key_list[3], (REPS, NTOK, KVW), 1.0, 6.0, ((0, 64), (1, 8)))
    first_moment = scatter_about(key_list[4], (REPS, D, KVW), 0.0003, 0.0018, ((0, 64), (1, 8)), jnp.float32)
    second_moment = jnp.clip(jnp.exp(math.log(2.0000000233721948e-07) - 2.3025851 * jax.random.uniform(key_list[5], (REPS, D, KVW), jnp.float32) ** steps_of(key_list[5], (REPS, D, KVW), ((0, 64), (1, 8)), -0.2, 0.2)), 1.999999987845058e-08, 2.0000000233721948e-07)
    return {"anchor": anchor, "momentum": momentum, "tokens": tokens, "targets": targets, "first_moment": first_moment, "second_moment": second_moment}


beta_one = 0.9
beta_two = 0.95
adam_eps = 1e-08
inner_rate = 0.2
decay_rate = 0.1
outer_rate = 0.7
outer_mom = 0.9

def replica_delta(start_full, rep_tokens, rep_targets, moment_first, moment_second):
    model_width = rep_tokens.shape[1]
    count_tokens = rep_tokens.shape[0]
    projected = jnp.dot(rep_tokens, start_full, preferred_element_type=jnp.float32) * model_width ** (-0.5)
    residual = (projected - rep_targets.astype(jnp.float32)).astype(jnp.bfloat16)
    token_blocks = rep_tokens.reshape(N_FSDP, count_tokens // N_FSDP, model_width)
    resid_blocks = residual.reshape(N_FSDP, count_tokens // N_FSDP, residual.shape[1])

    def accumulate(running, blocks):
        partial_term = lax.dot_general(blocks[0], blocks[1], (((0,), (0,)), ((), ())), preferred_element_type=jnp.float32)
        rounded = lax.optimization_barrier(partial_term.astype(jnp.bfloat16))
        return (running + rounded.astype(jnp.float32), None)
    summed, _ = lax.scan(accumulate, jnp.zeros((model_width, residual.shape[1]), jnp.float32), (token_blocks, resid_blocks))
    gradient = summed * (1.0 / (math.sqrt(model_width) * count_tokens))
    moment_one = beta_one * moment_first + (1.0 - beta_one) * gradient
    moment_two = beta_two * moment_second + (1.0 - beta_two) * gradient * gradient
    direction = moment_one / (jnp.sqrt(moment_two) + adam_eps)
    return inner_rate * (direction + decay_rate * start_full.astype(jnp.float32))

def reference(anchor, momentum, tokens, targets, first_moment, second_moment):
    start_full = anchor.astype(jnp.bfloat16)

    def over_replicas(running, items):
        return (running + replica_delta(start_full, items[0], items[1], items[2], items[3]), None)
    total, _ = lax.scan(over_replicas, jnp.zeros(anchor.shape, jnp.float32), (tokens, targets, first_moment, second_moment))
    mean_delta = total / N_REP
    momentum_next = outer_mom * momentum + mean_delta
    anchor_next = anchor - outer_rate * (mean_delta + outer_mom * momentum_next)
    return (anchor_next, momentum_next)
```

```python
import math

import jax
import jax.numpy as jnp
from jax import lax
from jax.sharding import Mesh, PartitionSpec as P

beta_one = 0.9
beta_two = 0.95
adam_eps = 1e-08
inner_rate = 0.2
decay_rate = 0.1
outer_rate = 0.7
outer_mom = 0.9

REP = ("zh", "y", "c")
FSDP = ("x", "zl")


def exchange(blocks, axes):
    return lax.all_to_all(blocks, axes, 0, 0)


def spread(block, axes):
    n = lax.axis_size(axes)
    return exchange(jnp.broadcast_to(block[None], (n,) + block.shape), axes)


def local(anchor, momentum, tokens, targets, first_moment, second_moment):
    groups = lax.axis_size(FSDP)
    replicas = lax.axis_size(REP)
    rows, owned = anchor.shape
    count, width = tokens.shape[1:]
    columns = targets.shape[2]

    own = anchor.astype(jnp.bfloat16).T
    wide = spread(own, FSDP)
    wide = wide.transpose(1, 0, 2).reshape(owned, width)
    part = spread(wide, ("zh", "c"))
    full = lax.all_gather(part, "y", axis=0)
    sizes = tuple(lax.axis_size(a) for a in REP)
    full = full.reshape(sizes[1], sizes[0], sizes[2], owned, width)
    full = full.transpose(1, 0, 2, 3, 4).reshape(columns, width)

    mine = exchange(tokens[0].reshape(count, groups, rows).transpose(1, 0, 2), FSDP)
    mine = mine.reshape(groups * count, rows)

    projected = lax.dot_general(
        tokens[0], full, (((1,), (1,)), ((), ())), preferred_element_type=jnp.float32
    )
    projected = projected * width ** (-0.5)
    residual = (projected - targets[0].astype(jnp.float32)).astype(jnp.bfloat16)
    residual = spread(residual, FSDP).reshape(groups * count, columns)

    summed = lax.dot_general(
        residual, mine, (((0,), (0,)), ((), ())), preferred_element_type=jnp.float32
    )
    gradient = summed * (1.0 / (math.sqrt(width) * groups * count))
    moment_one = beta_one * first_moment[0].T + (1.0 - beta_one) * gradient
    moment_two = beta_two * second_moment[0].T + (1.0 - beta_two) * gradient * gradient
    direction = moment_one / (jnp.sqrt(moment_two) + adam_eps)
    sent = direction.astype(jnp.bfloat16).reshape(replicas, owned, rows)
    total = jnp.sum(exchange(sent, REP).astype(jnp.float32), axis=0).T

    start = anchor.astype(jnp.bfloat16).astype(jnp.float32)
    mean_delta = inner_rate * (total / replicas + decay_rate * start)
    momentum_next = outer_mom * momentum + mean_delta
    anchor_next = anchor - outer_rate * (mean_delta + outer_mom * momentum_next)
    return (anchor_next, momentum_next)


def solution(mesh):
    fine = Mesh(mesh.devices.reshape(4, 8, 2, 4, 2), REP + FSDP)
    outer = P(FSDP, REP)
    inner = P(REP, FSDP, None)
    return jax.shard_map(
        local,
        mesh=fine,
        in_specs=(outer, outer, inner, inner, inner, inner),
        out_specs=(outer, outer),
        check_vma=False,
    )
```

```python
import math

import jax
import jax.numpy as jnp
from jax import lax
from jax.sharding import Mesh, PartitionSpec as P

beta_one = 0.9
beta_two = 0.95
adam_eps = 1e-08
inner_rate = 0.2
decay_rate = 0.1
outer_rate = 0.7
outer_mom = 0.9

REP = ("zh", "y", "c")
FSDP = ("x", "zl")


def exchange(blocks, axes):
    return lax.all_to_all(blocks, axes, 0, 0)


def spread(block, axes):
    n = lax.axis_size(axes)
    return exchange(jnp.broadcast_to(block[None], (n,) + block.shape), axes)


def local(anchor, momentum, tokens, targets, first_moment, second_moment):
    nx = lax.axis_size("x")
    groups = lax.axis_size(FSDP)
    replicas = lax.axis_size(REP)
    rows, owned = anchor.shape
    count, width = tokens.shape[1:]
    columns = targets.shape[2]
    at_x, at_zl = lax.axis_index("x"), lax.axis_index("zl")
    swap = [(0, 1), (1, 0)]

    own = anchor.astype(jnp.bfloat16).T
    pair = jnp.concatenate([own, lax.ppermute(own, "zl", swap)], axis=1)

    tok = tokens[0]

    def cut(x):
        first = lax.dynamic_slice_in_dim(tok, (2 * x + at_zl) * rows, rows, 1)
        second = lax.dynamic_slice_in_dim(tok, (2 * x + 1 - at_zl) * rows, rows, 1)
        return jnp.concatenate([first, second], axis=1)

    held = jnp.zeros((nx, count, 2 * rows), tok.dtype)
    for d in (2, 1, 3, 0):
        block = cut((at_x + d) % nx)
        if d:
            block = lax.ppermute(block, "x", [(i, (i + d) % nx) for i in range(nx)])
        held = lax.dynamic_update_slice_in_dim(held, block[None], (at_x - d) % nx, 0)
    held = held.reshape(nx * count, 2 * rows)

    start = spread(pair, REP).reshape(columns, 2 * rows)
    partial = lax.dot_general(
        held, start, (((1,), (1,)), ((), ())), preferred_element_type=jnp.float32
    ).astype(jnp.bfloat16)
    parts = exchange(partial.reshape(nx, count, columns), "x").astype(jnp.float32)
    projected = jnp.sum(parts, axis=0) * width ** (-0.5)
    residual = (projected - targets[0].astype(jnp.float32)).astype(jnp.bfloat16)
    residual = spread(residual, "x").reshape(nx * count, columns)

    def term(tok):
        return lax.dot_general(
            residual, tok, (((0,), (0,)), ((), ())), preferred_element_type=jnp.float32
        )

    other = lax.ppermute(term(held[:, rows:]).astype(jnp.bfloat16), "zl", swap)
    summed = term(held[:, :rows]) + other.astype(jnp.float32)
    gradient = summed * (1.0 / (math.sqrt(width) * groups * count))
    moment_one = beta_one * first_moment[0].T + (1.0 - beta_one) * gradient
    moment_two = beta_two * second_moment[0].T + (1.0 - beta_two) * gradient * gradient
    direction = moment_one / (jnp.sqrt(moment_two) + adam_eps)
    sent = direction.astype(jnp.bfloat16).reshape(replicas, owned, rows)
    total = jnp.sum(exchange(sent, REP).astype(jnp.float32), axis=0).T

    begin = anchor.astype(jnp.bfloat16).astype(jnp.float32)
    mean_delta = inner_rate * (total / replicas + decay_rate * begin)
    momentum_next = outer_mom * momentum + mean_delta
    anchor_next = anchor - outer_rate * (mean_delta + outer_mom * momentum_next)
    return (anchor_next, momentum_next)


def solution(mesh):
    fine = Mesh(mesh.devices.reshape(4, 8, 2, 4, 2), REP + FSDP)
    outer = P(FSDP, REP)
    inner = P(REP, FSDP, None)
    return jax.shard_map(
        local,
        mesh=fine,
        in_specs=(outer, outer, inner, inner, inner, inner),
        out_specs=(outer, outer),
        check_vma=False,
    )
```

```python
import math

import jax
import jax.numpy as jnp
from jax import lax
from jax.sharding import Mesh, PartitionSpec as P

beta_one = 0.9
beta_two = 0.95
adam_eps = 1e-08
inner_rate = 0.2
decay_rate = 0.1
outer_rate = 0.7
outer_mom = 0.9

REP = ("zh", "y", "c")
FSDP = ("x", "zl")
FAR = ("zh", "y")


def exchange(blocks, axes):
    return lax.all_to_all(blocks, axes, 0, 0)


def spread(block, axes):
    n = lax.axis_size(axes)
    return exchange(jnp.broadcast_to(block[None], (n,) + block.shape), axes)


def local(anchor, momentum, tokens, targets, first_moment, second_moment):
    nx = lax.axis_size("x")
    groups = lax.axis_size(FSDP)
    replicas = lax.axis_size(REP)
    rows, owned = anchor.shape
    count, width = tokens.shape[1:]
    columns = targets.shape[2]
    far = columns // owned // 2
    at_x, at_zl, at_c = lax.axis_index("x"), lax.axis_index("zl"), lax.axis_index("c")
    swap = [(0, 1), (1, 0)]

    def ordered(mine, other, at, axis):
        first = jnp.where(at == 0, mine, other)
        return jnp.stack([first, jnp.where(at == 0, other, mine)], axis)

    tok = tokens[0]
    held = jnp.zeros((nx, count, 2 * rows), tok.dtype)
    for d in (2, 1, 3, 0):
        block = lax.dynamic_slice_in_dim(tok, (at_x + d) % nx * 2 * rows, 2 * rows, 1)
        if d:
            block = lax.ppermute(block, "x", [(i, (i + d) % nx) for i in range(nx)])
        held = lax.dynamic_update_slice_in_dim(held, block[None], (at_x - d) % nx, 0)
    held = held.reshape(nx * count, 2 * rows)

    own = anchor.astype(jnp.bfloat16).T
    pair = ordered(own, lax.ppermute(own, "zl", swap), at_zl, 1).reshape(owned, 2 * rows)
    half = spread(pair, FAR)
    start = ordered(half, lax.ppermute(half, "c", swap), at_c, 1)
    start = start.reshape(columns, 2 * rows)

    partial = lax.dot_general(
        held, start, (((1,), (1,)), ((), ())), preferred_element_type=jnp.float32
    ).astype(jnp.bfloat16)
    parts = exchange(partial.reshape(nx, count, columns), "x").astype(jnp.float32)
    projected = jnp.sum(parts, axis=0) * width ** (-0.5)
    residual = (projected - targets[0].astype(jnp.float32)).astype(jnp.bfloat16)
    residual = spread(residual, "x").reshape(nx * count, columns)

    def term(at):
        return lax.dot_general(
            residual,
            lax.dynamic_slice_in_dim(held, at * rows, rows, 1),
            (((0,), (0,)), ((), ())),
            preferred_element_type=jnp.float32,
        )

    other = lax.ppermute(term(1 - at_zl).astype(jnp.bfloat16), "zl", swap)
    summed = term(at_zl) + other.astype(jnp.float32)
    gradient = summed * (1.0 / (math.sqrt(width) * groups * count))
    moment_one = beta_one * first_moment[0].T + (1.0 - beta_one) * gradient
    moment_two = beta_two * second_moment[0].T + (1.0 - beta_two) * gradient * gradient
    direction = moment_one / (jnp.sqrt(moment_two) + adam_eps)

    direction = direction.reshape(far, 2, owned, rows)
    given = lax.dynamic_index_in_dim(direction, 1 - at_c, 1, keepdims=False)
    kept = lax.dynamic_index_in_dim(direction, at_c, 1, keepdims=False)
    given = lax.ppermute(given.astype(jnp.bfloat16), "c", swap)
    sent = (kept + given.astype(jnp.float32)).astype(jnp.bfloat16)
    total = jnp.sum(exchange(sent, FAR).astype(jnp.float32), axis=0).T

    begin = anchor.astype(jnp.bfloat16).astype(jnp.float32)
    mean_delta = inner_rate * (total / replicas + decay_rate * begin)
    momentum_next = outer_mom * momentum + mean_delta
    anchor_next = anchor - outer_rate * (mean_delta + outer_mom * momentum_next)
    return (anchor_next, momentum_next)


def solution(mesh):
    fine = Mesh(mesh.devices.reshape(4, 8, 2, 4, 2), REP + FSDP)
    outer = P(FSDP, REP)
    inner = P(REP, FSDP, None)
    return jax.shard_map(
        local,
        mesh=fine,
        in_specs=(outer, outer, inner, inner, inner, inner),
        out_specs=(outer, outer),
        check_vma=False,
    )
```

```python
import math

import jax
import jax.numpy as jnp
from jax import lax
from jax.sharding import Mesh, PartitionSpec as P

beta_one = 0.9
beta_two = 0.95
adam_eps = 1e-08
inner_rate = 0.2
decay_rate = 0.1
outer_rate = 0.7
outer_mom = 0.9

REP = ("zh", "y", "c")
FSDP = ("x", "zl")
FAR = ("zh", "y")


def exchange(blocks, axes):
    return lax.all_to_all(blocks, axes, 0, 0)


def spread(block, axes):
    n = lax.axis_size(axes)
    return exchange(jnp.broadcast_to(block[None], (n,) + block.shape), axes)


def local(anchor, momentum, tokens, targets, first_moment, second_moment):
    nx = lax.axis_size("x")
    groups = lax.axis_size(FSDP)
    replicas = lax.axis_size(REP)
    rows, owned = anchor.shape
    count, width = tokens.shape[1:]
    columns = targets.shape[2]
    far = columns // owned // 2
    at_x, at_zl, at_c = lax.axis_index("x"), lax.axis_index("zl"), lax.axis_index("c")
    swap = [(0, 1), (1, 0)]

    own = anchor.astype(jnp.bfloat16).T
    half = spread(own, ("zl",) + FAR).reshape(2, far, owned, rows)
    other = lax.ppermute(half, "c", swap)
    first = jnp.where(at_c == 0, half, other)
    start = jnp.stack([first, jnp.where(at_c == 0, other, half)], 2)
    start = start.reshape(2, columns, rows)

    tok = tokens[0]
    held = jnp.zeros((nx, count, 2 * rows), tok.dtype)
    for d in (0, 2, 1, 3):
        block = lax.dynamic_slice_in_dim(tok, (at_x + d) % nx * 2 * rows, 2 * rows, 1)
        if d:
            block = lax.ppermute(block, "x", [(i, (i + d) % nx) for i in range(nx)])
        held = lax.dynamic_update_slice_in_dim(held, block[None], (at_x - d) % nx, 0)
    held = held.reshape(nx * count, 2 * rows)

    def project(at):
        return lax.dot_general(
            held[:, at * rows : (at + 1) * rows],
            start[at],
            (((1,), (1,)), ((), ())),
            preferred_element_type=jnp.float32,
        )

    partial = (project(0) + project(1)).astype(jnp.bfloat16)
    partial = partial.reshape(nx, count, columns)
    parts = exchange(partial, "x").astype(jnp.float32)
    projected = jnp.sum(parts, axis=0) * width ** (-0.5)
    residual = (projected - targets[0].astype(jnp.float32)).astype(jnp.bfloat16)
    residual = spread(residual, "x").reshape(nx * count, columns)

    def term(at):
        return lax.dot_general(
            residual,
            lax.dynamic_slice_in_dim(held, at * rows, rows, 1),
            (((0,), (0,)), ((), ())),
            preferred_element_type=jnp.float32,
        )

    other = lax.ppermute(term(1 - at_zl).astype(jnp.bfloat16), "zl", swap)
    kept = lax.optimization_barrier(term(at_zl))

    def direct(at):
        def of(a):
            a = a.reshape(far, 2, owned, rows)
            return lax.dynamic_index_in_dim(a, at, 1, keepdims=False)

        summed = of(kept) + of(other).astype(jnp.float32)
        gradient = summed * (1.0 / (math.sqrt(width) * groups * count))
        moment_one = beta_one * of(first_moment[0].T) + (1.0 - beta_one) * gradient
        squared = (1.0 - beta_two) * gradient * gradient
        moment_two = beta_two * of(second_moment[0].T) + squared
        return moment_one / (jnp.sqrt(moment_two) + adam_eps)

    given = lax.ppermute(direct(1 - at_c).astype(jnp.bfloat16), "c", swap)
    sent = (direct(at_c) + given.astype(jnp.float32)).astype(jnp.bfloat16)
    total = jnp.sum(exchange(sent, FAR).astype(jnp.float32), axis=0).T

    begin = anchor.astype(jnp.bfloat16).astype(jnp.float32)
    mean_delta = inner_rate * (total / replicas + decay_rate * begin)
    momentum_next = outer_mom * momentum + mean_delta
    anchor_next = anchor - outer_rate * (mean_delta + outer_mom * momentum_next)
    return (anchor_next, momentum_next)


def solution(mesh):
    fine = Mesh(mesh.devices.reshape(4, 8, 2, 4, 2), REP + FSDP)
    outer = P(FSDP, REP)
    inner = P(REP, FSDP, None)
    return jax.shard_map(
        local,
        mesh=fine,
        in_specs=(outer, outer, inner, inner, inner, inner),
        out_specs=(outer, outer),
        check_vma=False,
    )
```

```python
import math

import jax
import jax.numpy as jnp
from jax import lax
from jax.sharding import Mesh, PartitionSpec as P

beta_one = 0.9
beta_two = 0.95
adam_eps = 1e-08
inner_rate = 0.2
decay_rate = 0.1
outer_rate = 0.7
outer_mom = 0.9

REP = ("zh", "y", "c")
FSDP = ("x", "zl")
FAR = ("zh", "y")


def exchange(blocks, axes):
    return lax.all_to_all(blocks, axes, 0, 0)


def spread(block, axes):
    n = lax.axis_size(axes)
    return exchange(jnp.broadcast_to(block[None], (n,) + block.shape), axes)


def local(anchor, momentum, tokens, targets, first_moment, second_moment):
    nx = lax.axis_size("x")
    groups = lax.axis_size(FSDP)
    replicas = lax.axis_size(REP)
    rows, owned = anchor.shape
    count, width = tokens.shape[1:]
    columns = targets.shape[2]
    far = columns // owned // 2
    at_x, at_zl, at_c = lax.axis_index("x"), lax.axis_index("zl"), lax.axis_index("c")
    swap = [(0, 1), (1, 0)]

    own = anchor.astype(jnp.bfloat16).T
    half = spread(own, ("zl",) + FAR).reshape(2, far, owned, rows)
    other = lax.ppermute(half, "c", swap)
    first = jnp.where(at_c == 0, half, other)
    start = jnp.stack([first, jnp.where(at_c == 0, other, half)], 2)
    start = start.reshape(2, columns, rows)

    tok = tokens[0]
    right = [(i, (i + 1) % nx) for i in range(nx)]
    left = [(i, (i - 1) % nx) for i in range(nx)]

    def cut(x, first, size):
        at = (at_x + x) % nx * 2 * rows + first
        return lax.dynamic_slice_in_dim(tok, at, size, 1)

    def merge(*parts):
        return jnp.concatenate(parts, axis=1)

    from_left = lax.ppermute(merge(cut(1, 0, 2 * rows), cut(2, 0, rows)), "x", right)
    from_right = lax.ppermute(merge(cut(3, 0, 2 * rows), cut(2, rows, rows)), "x", left)
    far_left = lax.ppermute(from_left[:, 2 * rows :], "x", right)
    far_right = lax.ppermute(from_right[:, 2 * rows :], "x", left)

    held = jnp.zeros((nx, count, 2 * rows), tok.dtype)
    for d, first, block in (
        (0, 0, cut(0, 0, 2 * rows)),
        (3, 0, from_left[:, : 2 * rows]),
        (1, 0, from_right[:, : 2 * rows]),
        (2, 0, far_left),
        (2, rows, far_right),
    ):
        held = lax.dynamic_update_slice(held, block[None], ((at_x + d) % nx, 0, first))
    held = held.reshape(nx * count, 2 * rows)

    def project(at):
        return lax.dot_general(
            held[:, at * rows : (at + 1) * rows],
            start[at],
            (((1,), (1,)), ((), ())),
            preferred_element_type=jnp.float32,
        )

    partial = (project(0) + project(1)).astype(jnp.bfloat16)
    partial = partial.reshape(nx, count, columns)
    parts = exchange(partial, "x").astype(jnp.float32)
    projected = jnp.sum(parts, axis=0) * width ** (-0.5)
    residual = (projected - targets[0].astype(jnp.float32)).astype(jnp.bfloat16)
    residual = spread(residual, "x").reshape(nx * count, columns)

    def term(at):
        return lax.dot_general(
            residual,
            lax.dynamic_slice_in_dim(held, at * rows, rows, 1),
            (((0,), (0,)), ((), ())),
            preferred_element_type=jnp.float32,
        )

    other = lax.ppermute(term(1 - at_zl).astype(jnp.bfloat16), "zl", swap)
    kept = lax.optimization_barrier(term(at_zl))

    def direct(at):
        def of(a):
            a = a.reshape(far, 2, owned, rows)
            return lax.dynamic_index_in_dim(a, at, 1, keepdims=False)

        summed = of(kept) + of(other).astype(jnp.float32)
        gradient = summed * (1.0 / (math.sqrt(width) * groups * count))
        moment_one = beta_one * of(first_moment[0].T) + (1.0 - beta_one) * gradient
        squared = (1.0 - beta_two) * gradient * gradient
        moment_two = beta_two * of(second_moment[0].T) + squared
        return moment_one / (jnp.sqrt(moment_two) + adam_eps)

    given = lax.ppermute(direct(1 - at_c).astype(jnp.bfloat16), "c", swap)
    sent = (direct(at_c) + given.astype(jnp.float32)).astype(jnp.bfloat16)
    total = jnp.sum(exchange(sent, FAR).astype(jnp.float32), axis=0).T

    begin = anchor.astype(jnp.bfloat16).astype(jnp.float32)
    mean_delta = inner_rate * (total / replicas + decay_rate * begin)
    momentum_next = outer_mom * momentum + mean_delta
    anchor_next = anchor - outer_rate * (mean_delta + outer_mom * momentum_next)
    return (anchor_next, momentum_next)


def solution(mesh):
    fine = Mesh(mesh.devices.reshape(4, 8, 2, 4, 2), REP + FSDP)
    outer = P(FSDP, REP)
    inner = P(REP, FSDP, None)
    return jax.shard_map(
        local,
        mesh=fine,
        in_specs=(outer, outer, inner, inner, inner, inner),
        out_specs=(outer, outer),
        check_vma=False,
    )
```

```python
import math

import jax
import jax.numpy as jnp
from jax import lax
from jax.sharding import Mesh, PartitionSpec as P

beta_one = 0.9
beta_two = 0.95
adam_eps = 1e-08
inner_rate = 0.2
decay_rate = 0.1
outer_rate = 0.7
outer_mom = 0.9

REP = ("zh", "y", "c")
FSDP = ("x", "zl")
FAR = ("zh", "y")


def exchange(blocks, axes):
    return lax.all_to_all(blocks, axes, 0, 0)


def spread(block, axes):
    n = lax.axis_size(axes)
    return exchange(jnp.broadcast_to(block[None], (n,) + block.shape), axes)


def local(anchor, momentum, tokens, targets, first_moment, second_moment):
    nx = lax.axis_size("x")
    groups = lax.axis_size(FSDP)
    replicas = lax.axis_size(REP)
    rows, owned = anchor.shape
    count, width = tokens.shape[1:]
    columns = targets.shape[2]
    far = columns // owned // 2
    at_x, at_zl, at_c = lax.axis_index("x"), lax.axis_index("zl"), lax.axis_index("c")
    swap = [(0, 1), (1, 0)]

    def take(a, at, axis):
        start = [0] * a.ndim
        start[axis] = at
        size = [1 if i == axis else n for i, n in enumerate(a.shape)]
        return lax.dynamic_slice(a, start, size, allow_negative_indices=False)

    tok = tokens[0]
    right = [(i, (i + 1) % nx) for i in range(nx)]
    left = [(i, (i - 1) % nx) for i in range(nx)]

    def cut(x, zl):
        at = ((at_x + x) % nx * 2 + (at_zl + zl) % 2) * rows
        return lax.dynamic_slice(tok, (0, at), (count, rows), allow_negative_indices=False)

    def merge(*parts):
        return jnp.concatenate(parts, axis=1)

    from_left = lax.ppermute(merge(cut(1, 0), cut(1, 1), cut(2, 0)), "x", right)
    from_right = lax.ppermute(merge(cut(3, 0), cut(3, 1), cut(2, 1)), "x", left)
    far_left = lax.ppermute(from_left[:, 2 * rows :], "x", right)
    far_right = lax.ppermute(from_right[:, 2 * rows :], "x", left)

    held = jnp.zeros((nx, count, 2 * rows), tok.dtype)
    for d, first, block in (
        (0, 0, merge(cut(0, 0), cut(0, 1))),
        (3, 0, from_left[:, : 2 * rows]),
        (1, 0, from_right[:, : 2 * rows]),
        (2, 0, far_left),
        (2, rows, far_right),
    ):
        at = ((at_x + d) % nx, 0, first)
        held = lax.dynamic_update_slice(held, block[None], at, allow_negative_indices=False)
    held = held.reshape(nx * count, 2 * rows)

    own = anchor.astype(jnp.bfloat16).T
    half = spread(own, ("zl",) + FAR).reshape(2, far, owned, rows)
    swapped = lax.ppermute(half, "c", swap)

    first = jnp.where(at_c == 0, half, swapped)
    start = jnp.stack([first, jnp.where(at_c == 0, swapped, half)], 2)
    start = start.reshape(2, columns, rows)

    def project(first, at):
        return lax.dot_general(
            held[:, first : first + rows], take(start, at, 0)[0], (((1,), (1,)), ((), ())),
            preferred_element_type=jnp.float32,
        )

    partial = project(0, at_zl) + project(rows, 1 - at_zl)
    partial = partial.astype(jnp.bfloat16).reshape(nx, count, columns)
    parts = exchange(partial, "x").astype(jnp.float32)
    projected = jnp.sum(parts, axis=0) * width ** (-0.5)
    residual = (projected - targets[0].astype(jnp.float32)).astype(jnp.bfloat16)
    residual = spread(residual, "x").reshape(nx * count, columns)

    def term(first):
        return lax.dot_general(
            residual, held[:, first : first + rows], (((0,), (0,)), ((), ())),
            preferred_element_type=jnp.float32,
        )

    other = lax.ppermute(term(rows).astype(jnp.bfloat16), "zl", swap)
    kept = lax.optimization_barrier(term(0))

    def direct(at):
        def of(a):
            return take(a.reshape(far, 2, owned, rows), at, 1)[:, 0]

        summed = of(kept) + of(other).astype(jnp.float32)
        gradient = summed * (1.0 / (math.sqrt(width) * groups * count))
        moment_one = beta_one * of(first_moment[0].T) + (1.0 - beta_one) * gradient
        squared = (1.0 - beta_two) * gradient * gradient
        moment_two = beta_two * of(second_moment[0].T) + squared
        return moment_one / (jnp.sqrt(moment_two) + adam_eps)

    given = lax.ppermute(direct(1 - at_c).astype(jnp.bfloat16), "c", swap)
    kept = lax.optimization_barrier(direct(at_c))
    sent = (kept + given.astype(jnp.float32)).astype(jnp.bfloat16)
    total = jnp.sum(exchange(sent, FAR).astype(jnp.float32), axis=0).T

    begin = anchor.astype(jnp.bfloat16).astype(jnp.float32)
    mean_delta = inner_rate * (total / replicas + decay_rate * begin)
    momentum_next = outer_mom * momentum + mean_delta
    anchor_next = anchor - outer_rate * (mean_delta + outer_mom * momentum_next)
    return (anchor_next, momentum_next)


def solution(mesh):
    fine = Mesh(mesh.devices.reshape(4, 8, 2, 4, 2), REP + FSDP)
    outer = P(FSDP, REP)
    inner = P(REP, FSDP, None)
    return jax.shard_map(
        local,
        mesh=fine,
        in_specs=(outer, outer, inner, inner, inner, inner),
        out_specs=(outer, outer),
        check_vma=False,
    )
```

```python
import math

import jax
import jax.numpy as jnp
from jax import lax
from jax.sharding import Mesh, PartitionSpec as P

beta_one = 0.9
beta_two = 0.95
adam_eps = 1e-08
inner_rate = 0.2
decay_rate = 0.1
outer_rate = 0.7
outer_mom = 0.9

REP = ("zh", "y", "c")
FSDP = ("x", "zl")
FAR = ("zh", "y")


def exchange(blocks, axes):
    return lax.all_to_all(blocks, axes, 0, 0)


def spread(block, axes):
    n = lax.axis_size(axes)
    return exchange(jnp.broadcast_to(block[None], (n,) + block.shape), axes)


def local(anchor, momentum, tokens, targets, first_moment, second_moment):
    nx = lax.axis_size("x")
    groups = lax.axis_size(FSDP)
    replicas = lax.axis_size(REP)
    rows, owned = anchor.shape
    count, width = tokens.shape[1:]
    columns = targets.shape[2]
    far = columns // owned // 2
    at_x, at_zl, at_c = lax.axis_index("x"), lax.axis_index("zl"), lax.axis_index("c")
    swap = [(0, 1), (1, 0)]

    def take(a, at, axis):
        start = [0] * a.ndim
        start[axis] = at
        size = [1 if i == axis else n for i, n in enumerate(a.shape)]
        return lax.dynamic_slice(a, start, size, allow_negative_indices=False)

    tok = tokens[0]
    right = [(i, (i + 1) % nx) for i in range(nx)]
    left = [(i, (i - 1) % nx) for i in range(nx)]

    def cut(x, zl):
        at = ((at_x + x) % nx * 2 + (at_zl + zl) % 2) * rows
        return lax.dynamic_slice(tok, (0, at), (count, rows), allow_negative_indices=False)

    def merge(*parts):
        return jnp.concatenate(parts, axis=1)

    from_left = lax.ppermute(merge(cut(1, 0), cut(1, 1), cut(2, 0)), "x", right)
    from_right = lax.ppermute(merge(cut(3, 0), cut(3, 1), cut(2, 1)), "x", left)
    far_left = lax.ppermute(from_left[:, 2 * rows :], "x", right)
    far_right = lax.ppermute(from_right[:, 2 * rows :], "x", left)

    held = jnp.zeros((nx, count, 2 * rows), tok.dtype)
    for d, first, block in (
        (0, 0, merge(cut(0, 0), cut(0, 1))),
        (3, 0, from_left[:, : 2 * rows]),
        (1, 0, from_right[:, : 2 * rows]),
        (2, 0, far_left),
        (2, rows, far_right),
    ):
        at = ((at_x + d) % nx, 0, first)
        held = lax.dynamic_update_slice(held, block[None], at, allow_negative_indices=False)
    held = held.reshape(nx * count, 2 * rows)

    own = anchor.astype(jnp.bfloat16).T
    half = spread(own, ("zl",) + FAR).reshape(2, far, owned, rows)
    swapped = lax.ppermute(half, "c", swap)

    first = jnp.where(at_c == 0, half, swapped)
    start = jnp.stack([first, jnp.where(at_c == 0, swapped, half)], 2)
    start = start.reshape(2, columns, rows)

    def project(first, at):
        return lax.dot_general(
            held[:, first : first + rows], take(start, at, 0)[0], (((1,), (1,)), ((), ())),
            preferred_element_type=jnp.float32,
        )

    partial = project(0, at_zl) + project(rows, 1 - at_zl)
    partial = partial.astype(jnp.bfloat16).reshape(nx, count, columns)
    parts = exchange(partial, "x").astype(jnp.float32)
    projected = jnp.sum(parts, axis=0) * width ** (-0.5)
    residual = (projected - targets[0].astype(jnp.float32)).astype(jnp.bfloat16)
    residual = spread(residual, "x").reshape(nx * count, columns)

    def term(first):
        return lax.dot_general(
            residual, held[:, first : first + rows], (((0,), (0,)), ((), ())),
            preferred_element_type=jnp.float32,
        )

    def of(a, at):
        return take(a.reshape(far, 2, owned, rows), at, 1)[:, 0]

    lent = lax.optimization_barrier(term(rows))
    others = [
        lax.ppermute(of(lent, at).astype(jnp.bfloat16), "zl", swap)
        for at in (1 - at_c, at_c)
    ]
    kept = lax.optimization_barrier(term(0))

    def direct(at, other):
        summed = of(kept, at) + other.astype(jnp.float32)
        gradient = summed * (1.0 / (math.sqrt(width) * groups * count))
        moment_one = beta_one * of(first_moment[0].T, at) + (1.0 - beta_one) * gradient
        squared = (1.0 - beta_two) * gradient * gradient
        moment_two = beta_two * of(second_moment[0].T, at) + squared
        return moment_one / (jnp.sqrt(moment_two) + adam_eps)

    given = direct(1 - at_c, others[0]).astype(jnp.bfloat16)
    later, _ = lax.optimization_barrier((others[1], given))
    given = lax.ppermute(given, "c", swap)
    kept = lax.optimization_barrier(direct(at_c, later))
    sent = (kept + given.astype(jnp.float32)).astype(jnp.bfloat16)
    total = jnp.sum(exchange(sent, FAR).astype(jnp.float32), axis=0).T

    begin = anchor.astype(jnp.bfloat16).astype(jnp.float32)
    mean_delta = inner_rate * (total / replicas + decay_rate * begin)
    momentum_next = outer_mom * momentum + mean_delta
    anchor_next = anchor - outer_rate * (mean_delta + outer_mom * momentum_next)
    return (anchor_next, momentum_next)


def solution(mesh):
    fine = Mesh(mesh.devices.reshape(4, 8, 2, 4, 2), REP + FSDP)
    outer = P(FSDP, REP)
    inner = P(REP, FSDP, None)
    return jax.shard_map(
        local,
        mesh=fine,
        in_specs=(outer, outer, inner, inner, inner, inner),
        out_specs=(outer, outer),
        check_vma=False,
    )
```

```python
import math

import jax
import jax.numpy as jnp
from jax import lax
from jax.sharding import Mesh, PartitionSpec as P

beta_one = 0.9
beta_two = 0.95
adam_eps = 1e-08
inner_rate = 0.2
decay_rate = 0.1
outer_rate = 0.7
outer_mom = 0.9

REP = ("zh", "y", "c")
FSDP = ("x", "zl")
FAR = ("zh", "y")


def exchange(blocks, axes):
    return lax.all_to_all(blocks, axes, 0, 0)


def spread(block, axes):
    n = lax.axis_size(axes)
    return exchange(jnp.broadcast_to(block[None], (n,) + block.shape), axes)


def local(anchor, momentum, tokens, targets, first_moment, second_moment):
    nx = lax.axis_size("x")
    groups = lax.axis_size(FSDP)
    replicas = lax.axis_size(REP)
    rows, owned = anchor.shape
    count, width = tokens.shape[1:]
    columns = targets.shape[2]
    far = columns // owned // 2
    at_x, at_zl, at_c = lax.axis_index("x"), lax.axis_index("zl"), lax.axis_index("c")
    swap = [(0, 1), (1, 0)]

    def take(a, at, axis):
        start = [0] * a.ndim
        start[axis] = at
        size = [1 if i == axis else n for i, n in enumerate(a.shape)]
        return lax.dynamic_slice(a, start, size, allow_negative_indices=False)

    tok = tokens[0]
    right = [(i, (i + 1) % nx) for i in range(nx)]
    left = [(i, (i - 1) % nx) for i in range(nx)]

    def cut(x, zl):
        at = ((at_x + x) % nx * 2 + (at_zl + zl) % 2) * rows
        return lax.dynamic_slice(tok, (0, at), (count, rows), allow_negative_indices=False)

    def merge(*parts):
        return jnp.concatenate(parts, axis=1)

    from_left = lax.ppermute(merge(cut(1, 0), cut(1, 1)), "x", right)
    from_right = lax.ppermute(merge(cut(3, 0), cut(3, 1)), "x", left)
    after = 0 * (from_left[0, 0] + from_right[0, 0])
    across = merge(cut(2, 0), cut(2, 1)) + after
    across = lax.ppermute(across, "x", [(i, (i + 2) % nx) for i in range(nx)])

    held = jnp.zeros((nx, count, 2 * rows), tok.dtype)
    for d, block in (
        (0, merge(cut(0, 0), cut(0, 1))),
        (3, from_left),
        (1, from_right),
        (2, across),
    ):
        at = ((at_x + d) % nx, 0, 0)
        held = lax.dynamic_update_slice(held, block[None], at, allow_negative_indices=False)
    held = held.reshape(nx * count, 2 * rows)

    own = anchor.astype(jnp.bfloat16).T
    half = spread(own, ("zl",) + FAR).reshape(2, far, owned, rows)
    start = [lax.all_gather(half[i], "c", axis=1).reshape(columns, rows) for i in (0, 1)]
    start = jnp.stack(start)

    def project(first, at):
        return lax.dot_general(
            held[:, first : first + rows], take(start, at, 0)[0], (((1,), (1,)), ((), ())),
            preferred_element_type=jnp.float32,
        )

    partial = project(0, at_zl) + project(rows, 1 - at_zl)
    partial = partial.astype(jnp.bfloat16).reshape(nx, count, columns)
    parts = exchange(partial, "x").astype(jnp.float32)
    projected = jnp.sum(parts, axis=0) * width ** (-0.5)
    residual = (projected - targets[0].astype(jnp.float32)).astype(jnp.bfloat16)
    residual = spread(residual, "x").reshape(nx * count, columns)

    def term(first):
        return lax.dot_general(
            residual, held[:, first : first + rows], (((0,), (0,)), ((), ())),
            preferred_element_type=jnp.float32,
        )

    def of(a, at):
        return take(a.reshape(far, 2, owned, rows), at, 1)[:, 0]

    lent = lax.optimization_barrier(term(rows))
    others = [
        lax.ppermute(of(lent, at).astype(jnp.bfloat16), "zl", swap)
        for at in (1 - at_c, at_c)
    ]
    kept = lax.optimization_barrier(term(0))

    def direct(at, other):
        summed = of(kept, at) + other.astype(jnp.float32)
        gradient = summed * (1.0 / (math.sqrt(width) * groups * count))
        moment_one = beta_one * of(first_moment[0].T, at) + (1.0 - beta_one) * gradient
        squared = (1.0 - beta_two) * gradient * gradient
        moment_two = beta_two * of(second_moment[0].T, at) + squared
        return moment_one / (jnp.sqrt(moment_two) + adam_eps)

    given = direct(1 - at_c, others[0]).astype(jnp.bfloat16)
    later, _ = lax.optimization_barrier((others[1], given))
    given = lax.ppermute(given, "c", swap)
    kept = lax.optimization_barrier(direct(at_c, later))
    sent = (kept + given.astype(jnp.float32)).astype(jnp.bfloat16)
    total = jnp.sum(exchange(sent, FAR).astype(jnp.float32), axis=0).T

    begin = anchor.astype(jnp.bfloat16).astype(jnp.float32)
    mean_delta = inner_rate * (total / replicas + decay_rate * begin)
    momentum_next = outer_mom * momentum + mean_delta
    anchor_next = anchor - outer_rate * (mean_delta + outer_mom * momentum_next)
    return (anchor_next, momentum_next)


def solution(mesh):
    fine = Mesh(mesh.devices.reshape(4, 8, 2, 4, 2), REP + FSDP)
    outer = P(FSDP, REP)
    inner = P(REP, FSDP, None)
    return jax.shard_map(
        local,
        mesh=fine,
        in_specs=(outer, outer, inner, inner, inner, inner),
        out_specs=(outer, outer),
        check_vma=False,
    )
```

```python
import math

import jax
import jax.numpy as jnp
from jax import lax
from jax.sharding import Mesh, PartitionSpec as P

beta_one = 0.9
beta_two = 0.95
adam_eps = 1e-08
inner_rate = 0.2
decay_rate = 0.1
outer_rate = 0.7
outer_mom = 0.9

REP = ("zh", "y", "c")
FSDP = ("x", "zl")
FAR = ("zh", "y")


def exchange(blocks, axes):
    return lax.all_to_all(blocks, axes, 0, 0)


def spread(block, axes):
    n = lax.axis_size(axes)
    return exchange(jnp.broadcast_to(block[None], (n,) + block.shape), axes)


def local(anchor, momentum, tokens, targets, first_moment, second_moment):
    nx = lax.axis_size("x")
    groups = lax.axis_size(FSDP)
    replicas = lax.axis_size(REP)
    rows, owned = anchor.shape
    count, width = tokens.shape[1:]
    columns = targets.shape[2]
    far = columns // owned // 2
    at_x, at_zl, at_c = lax.axis_index("x"), lax.axis_index("zl"), lax.axis_index("c")
    swap = [(0, 1), (1, 0)]

    def take(a, at, axis):
        start = [0] * a.ndim
        start[axis] = at
        size = [1 if i == axis else n for i, n in enumerate(a.shape)]
        return lax.dynamic_slice(a, start, size, allow_negative_indices=False)

    tok = tokens[0]

    def cut(d):
        at = (at_x + d) % nx * 2 * rows
        size = (count, 2 * rows)
        return lax.dynamic_slice(tok, (0, at), size, allow_negative_indices=False)

    def shift(block, d):
        return lax.ppermute(block, "x", [(i, (i + d) % nx) for i in range(nx)])

    from_left = shift(cut(1), 1)
    from_right = shift(cut(3), 3)
    across = shift(cut(2) + 0 * (from_left + from_right), 2)

    held = jnp.zeros((nx, count, 2 * rows), tok.dtype)
    for d, block in ((0, cut(0)), (3, from_left), (1, from_right), (2, across)):
        at = ((at_x + d) % nx, 0, 0)
        held = lax.dynamic_update_slice(held, block[None], at, allow_negative_indices=False)
    held = held.reshape(nx * count, 2 * rows)

    own = anchor.astype(jnp.bfloat16).T
    half = spread(own, ("zl",) + FAR).reshape(2, far, owned, rows)
    start = [lax.all_gather(half[i], "c", axis=1).reshape(columns, rows) for i in (0, 1)]

    def project(i):
        return lax.dot_general(
            held[:, i * rows : (i + 1) * rows], start[i], (((1,), (1,)), ((), ())),
            preferred_element_type=jnp.float32,
        )

    partial = project(0) + project(1)
    partial = partial.astype(jnp.bfloat16).reshape(nx, count, columns)
    parts = exchange(partial, "x").astype(jnp.float32)
    projected = jnp.sum(parts, axis=0) * width ** (-0.5)
    residual = (projected - targets[0].astype(jnp.float32)).astype(jnp.bfloat16)
    residual = spread(residual, "x").reshape(nx * count, columns)

    def term(zl):
        met = (nx * count, rows)
        met = lax.dynamic_slice(held, (0, zl * rows), met, allow_negative_indices=False)
        return lax.dot_general(
            residual, met, (((0,), (0,)), ((), ())), preferred_element_type=jnp.float32
        )

    def of(a, at):
        return take(a.reshape(far, 2, owned, rows), at, 1)[:, 0]

    lent = lax.optimization_barrier(term(1 - at_zl))
    others = [
        lax.ppermute(of(lent, at).astype(jnp.bfloat16), "zl", swap)
        for at in (1 - at_c, at_c)
    ]
    kept = lax.optimization_barrier(term(at_zl))

    def direct(at, other):
        summed = of(kept, at) + other.astype(jnp.float32)
        gradient = summed * (1.0 / (math.sqrt(width) * groups * count))
        moment_one = beta_one * of(first_moment[0].T, at) + (1.0 - beta_one) * gradient
        squared = (1.0 - beta_two) * gradient * gradient
        moment_two = beta_two * of(second_moment[0].T, at) + squared
        return moment_one / (jnp.sqrt(moment_two) + adam_eps)

    given = direct(1 - at_c, others[0]).astype(jnp.bfloat16)
    later, _ = lax.optimization_barrier((others[1], given))
    given = lax.ppermute(given, "c", swap)
    kept = lax.optimization_barrier(direct(at_c, later))
    sent = (kept + given.astype(jnp.float32)).astype(jnp.bfloat16)
    total = jnp.sum(exchange(sent, FAR).astype(jnp.float32), axis=0).T

    begin = anchor.astype(jnp.bfloat16).astype(jnp.float32)
    mean_delta = inner_rate * (total / replicas + decay_rate * begin)
    momentum_next = outer_mom * momentum + mean_delta
    anchor_next = anchor - outer_rate * (mean_delta + outer_mom * momentum_next)
    return (anchor_next, momentum_next)


def solution(mesh):
    fine = Mesh(mesh.devices.reshape(4, 8, 2, 4, 2), REP + FSDP)
    outer = P(FSDP, REP)
    inner = P(REP, FSDP, None)
    return jax.shard_map(
        local,
        mesh=fine,
        in_specs=(outer, outer, inner, inner, inner, inner),
        out_specs=(outer, outer),
        check_vma=False,
    )
```

```python
import math

import jax
import jax.numpy as jnp
from jax import lax
from jax.sharding import Mesh, PartitionSpec as P

beta_one = 0.9
beta_two = 0.95
adam_eps = 1e-08
inner_rate = 0.2
decay_rate = 0.1
outer_rate = 0.7
outer_mom = 0.9

REP = ("zh", "y", "c")
FSDP = ("x", "zl")
FAR = ("zh", "y")


def exchange(blocks, axes):
    return lax.all_to_all(blocks, axes, 0, 0)


def spread(block, axes):
    n = lax.axis_size(axes)
    return exchange(jnp.broadcast_to(block[None], (n,) + block.shape), axes)


def local(anchor, momentum, tokens, targets, first_moment, second_moment):
    nx = lax.axis_size("x")
    groups = lax.axis_size(FSDP)
    replicas = lax.axis_size(REP)
    rows, owned = anchor.shape
    count, width = tokens.shape[1:]
    columns = targets.shape[2]
    far = columns // owned // 2
    at_x, at_zl, at_c = lax.axis_index("x"), lax.axis_index("zl"), lax.axis_index("c")
    swap = [(0, 1), (1, 0)]

    def take(a, at, axis):
        start = [0] * a.ndim
        start[axis] = at
        size = [1 if i == axis else n for i, n in enumerate(a.shape)]
        return lax.dynamic_slice(a, start, size, allow_negative_indices=False)

    tok = tokens[0]

    def cut(d):
        at = (at_x + d) % nx * 2 * rows
        size = (count, 2 * rows)
        return lax.dynamic_slice(tok, (0, at), size, allow_negative_indices=False)

    def shift(block, d):
        return lax.ppermute(block, "x", [(i, (i + d) % nx) for i in range(nx)])

    from_left = shift(cut(1), 1)
    from_right = shift(cut(3), 3)
    across = shift(cut(2) + 0 * (from_left + from_right), 2)

    held = jnp.zeros((nx, count, 2 * rows), tok.dtype)
    for d, block in ((0, cut(0)), (3, from_left), (1, from_right), (2, across)):
        at = ((at_x + d) % nx, 0, 0)
        held = lax.dynamic_update_slice(held, block[None], at, allow_negative_indices=False)
    held = held.reshape(nx * count, 2 * rows)

    own = anchor.astype(jnp.bfloat16).T
    half = spread(own, ("zl",) + FAR).reshape(2, far, owned, rows)
    start = [lax.all_gather(half[i], "c", axis=1).reshape(columns, rows) for i in (0, 1)]

    turned = [first_moment[0].T, second_moment[0].T]

    def project(i):
        return lax.dot_general(
            held[:, i * rows : (i + 1) * rows], start[i], (((1,), (1,)), ((), ())),
            preferred_element_type=jnp.float32,
        )

    partial = project(0) + project(1)
    offsets = (at_zl * rows, (1 - at_zl) * rows, 1 - at_c)
    first, second, offsets, partial = lax.optimization_barrier((*turned, offsets, partial))
    at_mine, at_other, not_c = offsets
    partial = partial.astype(jnp.bfloat16).reshape(nx, count, columns)
    parts = exchange(partial, "x").astype(jnp.float32)
    projected = jnp.sum(parts, axis=0) * width ** (-0.5)
    residual = (projected - targets[0].astype(jnp.float32)).astype(jnp.bfloat16)
    residual = spread(residual, "x").reshape(nx * count, columns)

    def term(at):
        met = (nx * count, rows)
        met = lax.dynamic_slice(held, (0, at), met, allow_negative_indices=False)
        return lax.dot_general(
            residual, met, (((0,), (0,)), ((), ())), preferred_element_type=jnp.float32
        )

    def of(a, at):
        return take(a.reshape(far, 2, owned, rows), at, 1)[:, 0]

    lent = lax.optimization_barrier(term(at_other))
    others = [
        lax.ppermute(of(lent, at).astype(jnp.bfloat16), "zl", swap)
        for at in (not_c, at_c)
    ]
    kept = lax.optimization_barrier(term(at_mine))

    def direct(at, other):
        summed = of(kept, at) + other.astype(jnp.float32)
        gradient = summed * (1.0 / (math.sqrt(width) * groups * count))
        moment_one = beta_one * of(first, at) + (1.0 - beta_one) * gradient
        squared = (1.0 - beta_two) * gradient * gradient
        moment_two = beta_two * of(second, at) + squared
        return moment_one / (jnp.sqrt(moment_two) + adam_eps)

    given = direct(not_c, others[0]).astype(jnp.bfloat16)
    later, _ = lax.optimization_barrier((others[1], given))
    given = lax.ppermute(given, "c", swap)
    kept = lax.optimization_barrier(direct(at_c, later))
    sent = (kept + given.astype(jnp.float32)).astype(jnp.bfloat16)
    total = jnp.sum(exchange(sent, FAR).astype(jnp.float32), axis=0).T

    begin = anchor.astype(jnp.bfloat16).astype(jnp.float32)
    mean_delta = inner_rate * (total / replicas + decay_rate * begin)
    momentum_next = outer_mom * momentum + mean_delta
    anchor_next = anchor - outer_rate * (mean_delta + outer_mom * momentum_next)
    return (anchor_next, momentum_next)


def solution(mesh):
    fine = Mesh(mesh.devices.reshape(4, 8, 2, 4, 2), REP + FSDP)
    outer = P(FSDP, REP)
    inner = P(REP, FSDP, None)
    return jax.shard_map(
        local,
        mesh=fine,
        in_specs=(outer, outer, inner, inner, inner, inner),
        out_specs=(outer, outer),
        check_vma=False,
    )
```

```python
import math

import jax
import jax.numpy as jnp
from jax import lax
from jax.sharding import Mesh, PartitionSpec as P

beta_one = 0.9
beta_two = 0.95
adam_eps = 1e-08
inner_rate = 0.2
decay_rate = 0.1
outer_rate = 0.7
outer_mom = 0.9

REP = ("zh", "y", "c")
FSDP = ("x", "zl")
FAR = ("zh", "y")


def exchange(blocks, axes):
    return lax.all_to_all(blocks, axes, 0, 0)


def spread(block, axes):
    n = lax.axis_size(axes)
    return exchange(jnp.broadcast_to(block[None], (n,) + block.shape), axes)


def local(anchor, momentum, tokens, targets, first_moment, second_moment):
    nx = lax.axis_size("x")
    groups = lax.axis_size(FSDP)
    replicas = lax.axis_size(REP)
    rows, owned = anchor.shape
    count, width = tokens.shape[1:]
    columns = targets.shape[2]
    far = columns // owned // 2
    at_x, at_zl, at_c = lax.axis_index("x"), lax.axis_index("zl"), lax.axis_index("c")
    swap = [(0, 1), (1, 0)]

    def take(a, at, axis):
        start = [0] * a.ndim
        start[axis] = at
        size = [1 if i == axis else n for i, n in enumerate(a.shape)]
        return lax.dynamic_slice(a, start, size, allow_negative_indices=False)

    tok = tokens[0]

    def cut(d):
        at = (at_x + d) % nx * 2 * rows
        size = (count, 2 * rows)
        return lax.dynamic_slice(tok, (0, at), size, allow_negative_indices=False)

    def shift(block, d):
        return lax.ppermute(block, "x", [(i, (i + d) % nx) for i in range(nx)])

    from_left = shift(cut(1), 1)
    from_right = shift(cut(3), 3)
    from_left, from_right = lax.optimization_barrier((from_left, from_right))
    across = shift(cut(2) + 0 * from_right, 2)

    held = jnp.zeros((nx, count, 2 * rows), tok.dtype)
    for d, block in ((0, cut(0)), (3, from_left), (1, from_right), (2, across)):
        at = ((at_x + d) % nx, 0, 0)
        held = lax.dynamic_update_slice(held, block[None], at, allow_negative_indices=False)
    held = held.reshape(nx * count, 2 * rows)

    own = anchor.astype(jnp.bfloat16).T
    half = spread(own, ("zl",) + FAR).reshape(2, far, owned, rows)
    start = [lax.all_gather(half[i], "c", axis=1).reshape(columns, rows) for i in (0, 1)]

    turned = [first_moment[0].T, second_moment[0].T]

    def project(i):
        return lax.dot_general(
            held[:, i * rows : (i + 1) * rows], start[i], (((1,), (1,)), ((), ())),
            preferred_element_type=jnp.float32,
        )

    partial = project(0) + project(1)
    offsets = (at_zl * rows, (1 - at_zl) * rows, 1 - at_c)
    first, second, offsets, partial = lax.optimization_barrier((*turned, offsets, partial))
    at_mine, at_other, not_c = offsets
    partial = partial.astype(jnp.bfloat16).reshape(nx, count, columns)
    parts = exchange(partial, "x").astype(jnp.float32)
    projected = jnp.sum(parts, axis=0) * width ** (-0.5)
    residual = (projected - targets[0].astype(jnp.float32)).astype(jnp.bfloat16)
    residual = spread(residual, "x").reshape(nx * count, columns)

    def term(at):
        met = (nx * count, rows)
        met = lax.dynamic_slice(held, (0, at), met, allow_negative_indices=False)
        return lax.dot_general(
            residual, met, (((0,), (0,)), ((), ())), preferred_element_type=jnp.float32
        )

    def of(a, at):
        return take(a.reshape(far, 2, owned, rows), at, 1)[:, 0]

    lent = lax.optimization_barrier(term(at_other))
    others = [
        lax.ppermute(of(lent, at).astype(jnp.bfloat16), "zl", swap)
        for at in (not_c, at_c)
    ]
    kept = lax.optimization_barrier(term(at_mine))

    def direct(at, other):
        summed = of(kept, at) + other.astype(jnp.float32)
        gradient = summed * (1.0 / (math.sqrt(width) * groups * count))
        moment_one = beta_one * of(first, at) + (1.0 - beta_one) * gradient
        squared = (1.0 - beta_two) * gradient * gradient
        moment_two = beta_two * of(second, at) + squared
        return moment_one / (jnp.sqrt(moment_two) + adam_eps)

    given = direct(not_c, others[0]).astype(jnp.bfloat16)
    later, _ = lax.optimization_barrier((others[1], given))
    given = lax.ppermute(given, "c", swap)
    kept = lax.optimization_barrier(direct(at_c, later))
    sent = (kept + given.astype(jnp.float32)).astype(jnp.bfloat16)
    total = jnp.sum(exchange(sent, FAR).astype(jnp.float32), axis=0).T

    begin = anchor.astype(jnp.bfloat16).astype(jnp.float32)
    mean_delta = inner_rate * (total / replicas + decay_rate * begin)
    momentum_next = outer_mom * momentum + mean_delta
    anchor_next = anchor - outer_rate * (mean_delta + outer_mom * momentum_next)
    return (anchor_next, momentum_next)


def solution(mesh):
    fine = Mesh(mesh.devices.reshape(4, 8, 2, 4, 2), REP + FSDP)
    outer = P(FSDP, REP)
    inner = P(REP, FSDP, None)
    return jax.shard_map(
        local,
        mesh=fine,
        in_specs=(outer, outer, inner, inner, inner, inner),
        out_specs=(outer, outer),
        check_vma=False,
    )
```

```python
import math

import jax
import jax.numpy as jnp
from jax import lax
from jax.sharding import Mesh, PartitionSpec as P

beta_one = 0.9
beta_two = 0.95
adam_eps = 1e-08
inner_rate = 0.2
decay_rate = 0.1
outer_rate = 0.7
outer_mom = 0.9

REP = ("zh", "y", "c")
FSDP = ("x", "zl")
FAR = ("zh", "y")


def exchange(blocks, axes):
    return lax.all_to_all(blocks, axes, 0, 0)


def spread(block, axes):
    n = lax.axis_size(axes)
    return exchange(jnp.broadcast_to(block[None], (n,) + block.shape), axes)


def local(anchor, momentum, tokens, targets, first_moment, second_moment):
    nx = lax.axis_size("x")
    groups = lax.axis_size(FSDP)
    replicas = lax.axis_size(REP)
    rows, owned = anchor.shape
    count, width = tokens.shape[1:]
    columns = targets.shape[2]
    far = columns // owned // 2
    at_x, at_zl, at_c = lax.axis_index("x"), lax.axis_index("zl"), lax.axis_index("c")
    swap = [(0, 1), (1, 0)]

    def take(a, at, axis):
        start = [0] * a.ndim
        start[axis] = at
        size = [1 if i == axis else n for i, n in enumerate(a.shape)]
        return lax.dynamic_slice(a, start, size, allow_negative_indices=False)

    tok = tokens[0]

    def cut(d):
        at = (at_x + d) % nx * 2 * rows
        size = (count, 2 * rows)
        return lax.dynamic_slice(tok, (0, at), size, allow_negative_indices=False)

    def shift(block, d):
        return lax.ppermute(block, "x", [(i, (i + d) % nx) for i in range(nx)])

    from_left = shift(cut(1), 1)
    from_right = shift(cut(3), 3)
    across = shift(cut(2) + 0 * (from_left + from_right), 2)

    held = jnp.zeros((nx, count, 2 * rows), tok.dtype)
    for d, block in ((0, cut(0)), (3, from_left), (1, from_right), (2, across)):
        at = ((at_x + d) % nx, 0, 0)
        held = lax.dynamic_update_slice(held, block[None], at, allow_negative_indices=False)
    held = held.reshape(nx * count, 2 * rows)

    own = anchor.astype(jnp.bfloat16).T
    half = spread(own, ("zl",) + FAR).reshape(2, far, owned, rows)
    other = lax.ppermute(half[0], "c", swap)
    first = jnp.where(at_c == 0, half[0], other)
    second = jnp.where(at_c == 0, other, half[0])
    start = [
        jnp.stack([first, second], 1).reshape(columns, rows),
        lax.all_gather(half[1], "c", axis=1).reshape(columns, rows),
    ]

    turned = [first_moment[0].T, second_moment[0].T]

    def project(i):
        return lax.dot_general(
            held[:, i * rows : (i + 1) * rows], start[i], (((1,), (1,)), ((), ())),
            preferred_element_type=jnp.float32,
        )

    partial = project(0) + project(1)
    offsets = (at_zl * rows, (1 - at_zl) * rows, 1 - at_c)
    first, second, offsets, partial = lax.optimization_barrier((*turned, offsets, partial))
    at_mine, at_other, not_c = offsets
    partial = partial.astype(jnp.bfloat16).reshape(nx, count, columns)
    parts = exchange(partial, "x").astype(jnp.float32)
    projected = jnp.sum(parts, axis=0) * width ** (-0.5)
    residual = (projected - targets[0].astype(jnp.float32)).astype(jnp.bfloat16)
    residual = spread(residual, "x").reshape(nx * count, columns)

    def term(at):
        met = (nx * count, rows)
        met = lax.dynamic_slice(held, (0, at), met, allow_negative_indices=False)
        return lax.dot_general(
            residual, met, (((0,), (0,)), ((), ())), preferred_element_type=jnp.float32
        )

    def of(a, at):
        return take(a.reshape(far, 2, owned, rows), at, 1)[:, 0]

    lent = lax.optimization_barrier(term(at_other))
    others = [
        lax.ppermute(of(lent, at).astype(jnp.bfloat16), "zl", swap)
        for at in (not_c, at_c)
    ]
    kept = lax.optimization_barrier(term(at_mine))

    def direct(at, other):
        summed = of(kept, at) + other.astype(jnp.float32)
        gradient = summed * (1.0 / (math.sqrt(width) * groups * count))
        moment_one = beta_one * of(first, at) + (1.0 - beta_one) * gradient
        squared = (1.0 - beta_two) * gradient * gradient
        moment_two = beta_two * of(second, at) + squared
        return moment_one / (jnp.sqrt(moment_two) + adam_eps)

    given = direct(not_c, others[0]).astype(jnp.bfloat16)
    later, _ = lax.optimization_barrier((others[1], given))
    given = lax.ppermute(given, "c", swap)
    kept = lax.optimization_barrier(direct(at_c, later))
    sent = (kept + given.astype(jnp.float32)).astype(jnp.bfloat16)
    total = jnp.sum(exchange(sent, FAR).astype(jnp.float32), axis=0).T

    begin = anchor.astype(jnp.bfloat16).astype(jnp.float32)
    mean_delta = inner_rate * (total / replicas + decay_rate * begin)
    momentum_next = outer_mom * momentum + mean_delta
    anchor_next = anchor - outer_rate * (mean_delta + outer_mom * momentum_next)
    return (anchor_next, momentum_next)


def solution(mesh):
    fine = Mesh(mesh.devices.reshape(4, 8, 2, 4, 2), REP + FSDP)
    outer = P(FSDP, REP)
    inner = P(REP, FSDP, None)
    return jax.shard_map(
        local,
        mesh=fine,
        in_specs=(outer, outer, inner, inner, inner, inner),
        out_specs=(outer, outer),
        check_vma=False,
    )
```
